32 devices in a mesh: groups: 2 (over x), row: 8 (over z, y), col: 2 (over core).
Axes of the slice: x: 2, y: 2, z: 4, core: 2. Of those that a mesh axis runs over, the one named last changes fastest.
Arguments:
- queries: bfloat16 [8192, 1024], P(('groups', 'row', 'col')), parts along dimension 0, may hold values from -200 to 200
- keys: bfloat16 [8192, 128], P(('groups', 'row', 'col')), parts along dimension 0, may hold values from -5 to 5
- values: bfloat16 [8192, 128], P(('groups', 'row', 'col')), parts along dimension 0, may hold values from -6 to 6
- doc_lengths: int32 [32], P('groups'), parts along dimension 0, may hold values from 1 to 3072, 4096 in all
Outputs:
- attended: bfloat16 [8192, 1024], P(('groups', 'row', 'col')), parts along dimension 0
The draws below stay inside these ranges and needn't reach their ends.
There are 2 independent parts, one for each index of `groups`. The reference program is written for one: setup_inputs(seed, part) draws one part's arguments, and reference() takes and returns one part's arrays. A program takes and returns all parts, laid end to end along the dimension named above; each array names one. Nothing has to cross between parts.
Inputs may be any that keep to these rules, and one draw needn't show every extreme that they name: `doc_lengths`: the 16 lengths sum to 4096 and the longest is exactly 3072.
All inputs are finite; a program needn't handle non-finite values.
Results may differ from the reference program's by a relative error of at most 0.0055.
Values may be sent and summed in bfloat16 or wider, within the bound.
A program may use at most 64 MiB of HBM per device.

```python
import math
import jax
import jax.numpy as jnp
import numpy as np
from jax import lax

HEADS = 8
HEAD_DIM = 128
DOCS = 16
SEQ = 4096
MAXDOC = 3072


def shared_pair(key):
    key_keys = jax.random.fold_in(key, 12)
    key_queries = jax.random.fold_in(key, 11)
    keymat = jnp.clip(jax.random.normal(key_keys, (SEQ, HEAD_DIM), jnp.float32), -4.0, 4.0)
    querymat = jnp.clip(jax.random.normal(key_queries, (SEQ, HEADS, HEAD_DIM), jnp.float32), -4.0, 4.0)
    places = jnp.arange(SEQ)
    half_back = jnp.roll(keymat, SEQ // 2, axis=0)
    picked = (places % 61 == 30) & (places >= SEQ // 2)
    querymat = jnp.where(picked[:, None, None], half_back[:, None, :] + 0.0 * querymat, querymat)
    return (querymat, keymat)


def draw_queries(key, part):
    querymat, keymat = shared_pair(key)
    return querymat.reshape(SEQ, HEADS * HEAD_DIM).astype(jnp.bfloat16)


def draw_keys(key, part):
    querymat, keymat = shared_pair(key)
    return keymat.astype(jnp.bfloat16)


def block_scale(own_key, extent, pieces, least, top_value):
    loudness, own = 1.0, jax.random.fold_in(own_key, 6)
    for dim, parts in pieces:
        steps = jnp.exp(jax.random.uniform(jax.random.fold_in(own, dim), (parts,), jnp.float32, least / len(pieces), top_value / len(pieces)))
        loudness = loudness * jnp.repeat(steps, extent[dim] // parts).reshape([-1 if axis == dim else 1 for axis in range(len(extent))])
    return loudness


def length_profile(number_of, total, reach, slope):
    loads = [(1 << 20) // math.isqrt(standing ** slope) + 1 for standing in range(2, number_of + 1)]
    spare, holding = total - reach - (number_of - 1), [1] * (number_of - 1)
    while spare > 0:
        candidates = [i for i in range(number_of - 1) if holding[i] < reach]
        mass, left = sum([loads[i] for i in candidates]), spare
        for i in candidates:
            addition = min(reach - holding[i], max(1, left * loads[i] // mass), spare)
            holding[i] = holding[i] + addition
            spare = spare - addition
    return np.array([reach] + holding)


def uneven(own_key, amount, total, limit, lean):
    if amount == 2:
        one = jax.random.randint(own_key, (), max(1, total - limit), min(limit, total - 1) + 1)
        return jnp.stack([one, total - one])
    tallies = jnp.asarray(length_profile(amount, total, limit, lean), jnp.int32)
    twos = (amount - 1) // 2
    donor, taker = tallies[1:1 + 2 * twos:2], tallies[2:2 + 2 * twos:2]
    margin = jnp.minimum(donor - 1, limit - taker)
    moved = jax.random.randint(jax.random.fold_in(own_key, 1), (twos,), 0, 1 << 20) % (margin + 1)
    tallies = tallies.at[1:1 + 2 * twos:2].set(donor - moved).at[2:2 + 2 * twos:2].set(taker + moved)
    return tallies[jax.random.permutation(jax.random.fold_in(own_key, 2), amount)]


def gaussian(stream_key, extent, width, most, split=(), kind=jnp.bfloat16):
    array = width * jax.random.normal(stream_key, extent, jnp.float32)
    if split:
        array = array * block_scale(stream_key, extent, split, -0.22, 0.18)
    return jnp.clip(array, -most, most).astype(kind)


def setup_inputs(seed: int = 0, part: int = 0) -> dict:
    key_of = jax.random.split(jax.random.key(seed), 5)
    part_splits = jax.random.split(jax.random.fold_in(key_of[4], part), 5)
    return {
        "queries": draw_queries(jax.random.fold_in(jax.random.fold_in(key_of[4], part), 71), part),
        "keys": draw_keys(jax.random.fold_in(jax.random.fold_in(key_of[4], part), 71), part),
        "values": gaussian(part_splits[2], (SEQ, HEAD_DIM), 1.0, 6.0, ((0, 16),)),
        "doc_lengths": uneven(part_splits[3], DOCS, SEQ, MAXDOC, 2).astype(jnp.int32),
    }


def reference(queries, keys, values, doc_lengths):
    ends = jnp.cumsum(doc_lengths).astype(jnp.int32)
    places = jnp.arange(SEQ, dtype=jnp.int32)
    owner = jnp.sum((places[:, None] >= ends[None, :]).astype(jnp.int32), axis=1)
    qmat = queries.reshape(SEQ, HEADS, HEAD_DIM).astype(jnp.float32)
    kmat = keys.astype(jnp.float32)
    value_matrix = values.astype(jnp.float32)
    block = math.gcd(SEQ, 512)
    scale = HEAD_DIM ** -0.5

    def one_block(index):
        first = (index * block).astype(jnp.int32)
        qpart = lax.dynamic_slice_in_dim(qmat, first, block, 0)
        qpos = first + jnp.arange(block, dtype=jnp.int32)
        qdoc = lax.dynamic_slice_in_dim(owner, first, block, 0)
        scores = jnp.einsum("qhd,kd->qhk", qpart, kmat, precision=lax.Precision.HIGHEST) * scale
        visible = (owner[None, :] == qdoc[:, None]) & (places[None, :] <= qpos[:, None])
        masked = jnp.where(visible[:, None, :], scores, jnp.float32(-1e30))
        top = jnp.max(masked, axis=-1)
        weights = jnp.where(visible[:, None, :], jnp.exp(scores - top[..., None]), jnp.float32(0.0))
        total = jnp.sum(weights, axis=-1)
        rounded_down_value = weights.astype(jnp.bfloat16).astype(jnp.float32)
        summed_values = jnp.einsum("uxa,ag->uxg", rounded_down_value, value_matrix, precision=lax.Precision.HIGHEST)
        return (summed_values / total[..., None]).astype(jnp.bfloat16)

    outcome = lax.map(one_block, jnp.arange(SEQ // block, dtype=jnp.int32))
    return outcome.reshape(SEQ, HEADS * HEAD_DIM)
```

```python
import functools

import jax
import jax.numpy as jnp
from jax import lax
from jax.experimental import pallas as pl
from jax.experimental.pallas import tpu as pltpu
from jax.sharding import PartitionSpec as P

HEAD_DIM = 128
RATE = HEAD_DIM ** (-0.5) * 1.4426950408889634
MASKED = -1e30


def kernel(
    n_row,
    n_col,
    lanes,
    reach,
    lens_ref,
    q_ref,
    k_ref,
    v_ref,
    o_ref,
    kbuf,
    vbuf,
    top_ref,
    total_ref,
    acc_ref,
    in_sem,
    mate_sem,
    up_send,
    cross_send,
    mate_send,
):
    shard = q_ref.shape[0]
    heads = q_ref.shape[1] // HEAD_DIM
    levels = n_row // lanes
    steps = 2 * (min(levels - 1, (reach + lanes - 1) // lanes) + 1)
    row = lax.axis_index("row")
    col = lax.axis_index("col")
    level = row // lanes
    lane = row % lanes
    mate = 1 - col
    other = level * lanes + (lanes - 1 - lane)
    mine = pl.ds(pl.multiple_of(col * shard, shard), shard)
    theirs = pl.ds(pl.multiple_of(mate * shard, shard), shard)

    def needs(reader, source):
        return (source >= 0) & (reader > source) & (reader - source <= reach)

    has_up = level + 1 < levels
    has_down = level > 0
    has_other = lanes > 1

    barrier = pltpu.get_barrier_semaphore()
    pl.semaphore_signal(barrier, inc=1, device_id={"col": mate})
    if has_other:
        pl.semaphore_signal(barrier, inc=1, device_id={"row": other})

    @pl.when(has_up)
    def _():
        pl.semaphore_signal(barrier, inc=1, device_id={"row": row + lanes})

    @pl.when(has_down)
    def _():
        pl.semaphore_signal(barrier, inc=1, device_id={"row": row - lanes})

    count = 1 + int(has_other) + has_up.astype(jnp.int32) + has_down.astype(jnp.int32)
    pl.semaphore_wait(barrier, count)

    def send(src, buf, source, which, j, sends, recvs, at, device):
        return pltpu.make_async_remote_copy(
            src_ref=src,
            dst_ref=buf.at[source, mine, :],
            send_sem=sends.at[which, j],
            recv_sem=recvs.at[which, at],
            device_id=device,
            device_id_type=pl.DeviceIdType.MESH,
        )

    def source_of(j):
        dist, kind = j // 2, j % 2
        cross = kind == 1
        from_lane = jnp.where(cross, lanes - 1 - lane, lane)
        source = (level - dist) * lanes + from_lane
        if lanes == 1:
            source = jnp.where(cross, -1, source)
        return source

    def relays(j, source, straight):
        mate_wants = (source < row) | (col < mate)
        found = [(mate_wants, mate_send, mate_sem, j, {"col": mate})]
        up = straight & has_up & needs(row + lanes, source)
        found.append((up, up_send, in_sem, j + 2, {"row": row + lanes}))
        if has_other:
            cross = straight & needs(other, source)
            found.append((cross, cross_send, in_sem, j + 1, {"row": other}))
        return found

    def forward(src, buf, source, which, j, straight):
        for wanted, sends, recvs, at, device in reversed(relays(j, source, straight)):

            @pl.when(wanted)
            def _():
                send(src, buf, source, which, j, sends, recvs, at, device).start()

    def arrived(buf, source, which, j, sems, part):
        here = buf.at[source, part, :]
        pltpu.make_async_copy(here, here, sems.at[which, j]).wait()

    forward(k_ref, kbuf, row, 0, 0, True)
    forward(v_ref, vbuf, row, 1, 0, True)

    first = (row * n_col + col) * shard
    qpos = first + lax.broadcasted_iota(jnp.int32, (1, shard), 1)
    begin = jnp.zeros((1, shard), jnp.int32)
    end = jnp.int32(0)
    for doc in range(lens_ref.shape[0]):
        length = lens_ref[doc]
        end = end + length
        begin = begin + jnp.where(qpos >= end, length, 0)

    def attend(kblock, vblock, kfirst, fresh):
        count = kblock.shape[0]
        kpos = kfirst + lax.broadcasted_iota(jnp.int32, (count, shard), 0)
        seen = kpos >= begin
        if fresh:
            seen = seen & (kpos <= qpos)
        bias = jnp.where(seen, jnp.float32(0.0), jnp.float32(MASKED))
        vflip = vblock.T
        for head in range(heads):
            qhead = q_ref[:, head * HEAD_DIM : (head + 1) * HEAD_DIM]
            scores = lax.dot_general(
                kblock, qhead, (((1,), (1,)), ((), ())), preferred_element_type=jnp.float32
            )
            scores = scores + bias
            top = jnp.max(scores, axis=0, keepdims=True)
            if not fresh:
                before = top_ref[head : head + 1, :]
                top = jnp.maximum(before, top)
            weights = jnp.exp2((scores - top) * RATE)
            total = jnp.sum(weights, axis=0, keepdims=True)
            summed = jnp.dot(
                vflip, weights.astype(jnp.bfloat16), preferred_element_type=jnp.float32
            )
            if not fresh:
                factor = jnp.exp2((before - top) * RATE)
                total = total + total_ref[head : head + 1, :] * factor
                summed = summed + acc_ref[head] * factor
            top_ref[head : head + 1, :] = top
            total_ref[head : head + 1, :] = total
            acc_ref[head] = summed

    attend(k_ref[...], v_ref[...], first, True)

    @pl.when(col > 0)
    def _():
        arrived(kbuf, row, 0, 0, mate_sem, theirs)
        arrived(vbuf, row, 1, 0, mate_sem, theirs)
        attend(kbuf[row, :shard, :], vbuf[row, :shard, :], row * n_col * shard, False)

    @pl.loop(1, steps)
    def _(j):
        source = source_of(j)

        @pl.when(needs(row, source))
        def _():
            straight = j % 2 == 0
            for which, buf in enumerate((kbuf, vbuf)):
                arrived(buf, source, which, j, in_sem, mine)
                forward(buf.at[source, mine, :], buf, source, which, j, straight)
            arrived(kbuf, source, 0, j, mate_sem, theirs)
            arrived(vbuf, source, 1, j, mate_sem, theirs)
            attend(kbuf[source], vbuf[source], source * n_col * shard, False)

    for head in range(heads):
        inverse = 1.0 / total_ref[head : head + 1, :]
        result = (acc_ref[head] * inverse).T
        o_ref[:, head * HEAD_DIM : (head + 1) * HEAD_DIM] = result.astype(o_ref.dtype)

    @pl.loop(0, steps)
    def _(j):
        source = source_of(j)

        @pl.when(needs(row, source) | (j == 0))
        def _():
            for wanted, sends, recvs, at, device in relays(j, source, j % 2 == 0):

                @pl.when(wanted)
                def _():
                    for which, buf in enumerate((kbuf, vbuf)):
                        part = buf.at[source, mine, :]
                        send(part, buf, source, which, j, sends, recvs, at, device).wait_send()


def shards(n_row, n_col, queries, keys, values, doc_lengths):
    shard, width = queries.shape
    lanes = 2 if n_row % 2 == 0 else 1
    span = shard * n_row * n_col
    longest = (3 * span) // 4
    reach = min(n_row - 1, -(-longest // (shard * n_col)))
    levels = n_row // lanes
    steps = 2 * (min(levels - 1, (reach + lanes - 1) // lanes) + 1)
    tile = shard * n_col
    heads = width // HEAD_DIM
    vmem = pl.BlockSpec(memory_space=pltpu.VMEM)
    sems = pltpu.SemaphoreType.DMA((2, steps))
    return pl.pallas_call(
        functools.partial(kernel, n_row, n_col, lanes, reach),
        out_shape=jax.ShapeDtypeStruct(queries.shape, queries.dtype),
        in_specs=[pl.BlockSpec(memory_space=pltpu.SMEM), vmem, vmem, vmem],
        out_specs=vmem,
        scratch_shapes=[
            pltpu.VMEM((n_row, tile, HEAD_DIM), keys.dtype),
            pltpu.VMEM((n_row, tile, HEAD_DIM), values.dtype),
            pltpu.VMEM((heads, shard), jnp.float32),
            pltpu.VMEM((heads, shard), jnp.float32),
            pltpu.VMEM((heads, HEAD_DIM, shard), jnp.float32),
            sems,
            sems,
            sems,
            sems,
            sems,
        ],
        compiler_params=pltpu.CompilerParams(
            collective_id=0, has_side_effects=True, vmem_limit_bytes=60 << 20
        ),
        name="attend",
    )(doc_lengths, queries, keys, values)


def solution(mesh):
    placed = P(("groups", "row", "col"), None)
    return jax.shard_map(
        functools.partial(shards, mesh.shape["row"], mesh.shape["col"]),
        mesh=mesh,
        in_specs=(placed, placed, placed, P("groups")),
        out_specs=placed,
        check_vma=False,
    )
```

```python
import functools

import jax
import jax.numpy as jnp
from jax import lax
from jax.experimental import pallas as pl
from jax.experimental.pallas import tpu as pltpu
from jax.sharding import PartitionSpec as P

HEAD_DIM = 128
RATE = HEAD_DIM ** (-0.5) * 1.4426950408889634
MASKED = -1e30


def kernel(
    n_row,
    n_col,
    lanes,
    reach,
    lens_ref,
    q_ref,
    k_ref,
    v_ref,
    o_ref,
    kbuf,
    vbuf,
    top_ref,
    total_ref,
    acc_ref,
    qa_ref,
    s_ref,
    load_sem,
    in_sem,
    mate_sem,
    up_send,
    cross_send,
    mate_send,
):
    shard = q_ref.shape[0]
    heads = q_ref.shape[1] // HEAD_DIM
    levels = n_row // lanes
    steps = 2 * (min(levels - 1, (reach + lanes - 1) // lanes) + 1)
    row = lax.axis_index("row")
    col = lax.axis_index("col")
    level = row // lanes
    lane = row % lanes
    mate = 1 - col
    other = level * lanes + (lanes - 1 - lane)
    mine = pl.ds(pl.multiple_of(col * shard, shard), shard)
    theirs = pl.ds(pl.multiple_of(mate * shard, shard), shard)

    def needs(reader, source):
        return (source >= 0) & (reader > source) & (reader - source <= reach)

    has_up = level + 1 < levels
    has_down = level > 0
    has_other = lanes > 1

    barrier = pltpu.get_barrier_semaphore()
    pl.semaphore_signal(barrier, inc=1, device_id={"col": mate})
    if has_other:
        pl.semaphore_signal(barrier, inc=1, device_id={"row": other})

    @pl.when(has_up)
    def _():
        pl.semaphore_signal(barrier, inc=1, device_id={"row": row + lanes})

    @pl.when(has_down)
    def _():
        pl.semaphore_signal(barrier, inc=1, device_id={"row": row - lanes})

    loads = [
        pltpu.make_async_copy(k_ref, kbuf.at[row, mine, :], load_sem.at[0]),
        pltpu.make_async_copy(v_ref, vbuf.at[row, mine, :], load_sem.at[1]),
    ]
    for head in range(heads):
        part = q_ref.at[:, head * HEAD_DIM : (head + 1) * HEAD_DIM]
        loads.append(
            pltpu.make_async_copy(part, qa_ref.at[head, :, :HEAD_DIM], load_sem.at[2 + head])
        )
    for load in loads:
        load.start()

    count = 1 + int(has_other) + has_up.astype(jnp.int32) + has_down.astype(jnp.int32)
    pl.semaphore_wait(barrier, count)

    def send(src, buf, source, which, j, sends, recvs, at, device):
        return pltpu.make_async_remote_copy(
            src_ref=src,
            dst_ref=buf.at[source, mine, :],
            send_sem=sends.at[which, j],
            recv_sem=recvs.at[which, at],
            device_id=device,
            device_id_type=pl.DeviceIdType.MESH,
        )

    def source_of(j):
        dist, kind = j // 2, j % 2
        cross = kind == 1
        from_lane = jnp.where(cross, lanes - 1 - lane, lane)
        source = (level - dist) * lanes + from_lane
        if lanes == 1:
            source = jnp.where(cross, -1, source)
        return source

    def relays(j, source, straight):
        mate_wants = (source < row) | (col < mate)
        found = [(mate_wants, mate_send, mate_sem, j, {"col": mate})]
        up = straight & has_up & needs(row + lanes, source)
        found.append((up, up_send, in_sem, j + 2, {"row": row + lanes}))
        if has_other:
            cross = straight & needs(other, source)
            found.append((cross, cross_send, in_sem, j + 1, {"row": other}))
        return found

    def forward(src, buf, source, which, j, straight):
        for wanted, sends, recvs, at, device in reversed(relays(j, source, straight)):

            @pl.when(wanted)
            def _():
                send(src, buf, source, which, j, sends, recvs, at, device).start()

    def arrived(buf, source, which, j, sems, part):
        here = buf.at[source, part, :]
        pltpu.make_async_copy(here, here, sems.at[which, j]).wait()

    forward(k_ref, kbuf, row, 0, 0, True)
    forward(v_ref, vbuf, row, 1, 0, True)

    first = (row * n_col + col) * shard
    qpos = first + lax.broadcasted_iota(jnp.int32, (1, shard), 1)

    def within(places):
        return (places >= begins) & (places < ends)

    lanes_of = lax.broadcasted_iota(jnp.int32, (1, HEAD_DIM), 1)
    begins = jnp.zeros((1, HEAD_DIM), jnp.int32)
    ends = jnp.full((1, HEAD_DIM), n_row * n_col * shard, jnp.int32)
    end = jnp.int32(0)
    docs = lens_ref.shape[0]
    for doc in range(docs):
        begins = jnp.where(lanes_of == doc, end, begins)
        end = end + lens_ref[doc]
        ends = jnp.where(lanes_of == doc, end, ends)
    qplace = first + lax.broadcasted_iota(jnp.int32, (shard, HEAD_DIM), 0)
    member = jnp.where(within(qplace) & (lanes_of < docs), 1.0, 0.0).astype(jnp.bfloat16)
    for head in range(heads):
        qa_ref[head, :, HEAD_DIM:] = member
    for load in loads:
        load.wait()

    def attend(kblock, vblock, kfirst, fresh):
        count = kblock.shape[0]
        kplace = kfirst + lax.broadcasted_iota(jnp.int32, (count, HEAD_DIM), 0)
        apart = jnp.where(within(kplace), 0.0, MASKED).astype(jnp.bfloat16)
        kwide = jnp.concatenate([kblock, apart], axis=1)
        if fresh:
            kpos = kfirst + lax.broadcasted_iota(jnp.int32, (count, shard), 0)
            bias = jnp.where(kpos <= qpos, jnp.float32(0.0), jnp.float32(MASKED))
        vflip = vblock.T

        def score(head):
            scores = lax.dot_general(
                kwide, qa_ref[head], (((1,), (1,)), ((), ())), preferred_element_type=jnp.float32
            )
            if fresh:
                scores = scores + bias
            s_ref[head % 2, :count, :] = scores
            top = jnp.max(scores, axis=0, keepdims=True)
            if fresh:
                return top, top
            before = top_ref[head : head + 1, :]
            return before, jnp.maximum(before, top)

        ahead = score(0)
        for head in range(heads):
            before, top = ahead
            if head + 1 < heads:
                ahead = score(head + 1)
            weights = jnp.exp2((s_ref[head % 2, :count, :] - top) * RATE)
            total = jnp.sum(weights, axis=0, keepdims=True)
            summed = jnp.dot(
                vflip, weights.astype(jnp.bfloat16), preferred_element_type=jnp.float32
            )
            if not fresh:
                factor = jnp.exp2((before - top) * RATE)
                total = total + total_ref[head : head + 1, :] * factor
                summed = summed + acc_ref[head] * factor
            top_ref[head : head + 1, :] = top
            total_ref[head : head + 1, :] = total
            acc_ref[head] = summed

    attend(kbuf[row, mine, :], vbuf[row, mine, :], first, True)

    @pl.when(col > 0)
    def _():
        arrived(kbuf, row, 0, 0, mate_sem, theirs)
        arrived(vbuf, row, 1, 0, mate_sem, theirs)
        attend(kbuf[row, :shard, :], vbuf[row, :shard, :], row * n_col * shard, False)

    @pl.loop(1, steps)
    def _(j):
        source = source_of(j)

        @pl.when(needs(row, source))
        def _():
            straight = j % 2 == 0
            for which, buf in enumerate((kbuf, vbuf)):
                arrived(buf, source, which, j, in_sem, mine)
                forward(buf.at[source, mine, :], buf, source, which, j, straight)
            arrived(kbuf, source, 0, j, mate_sem, theirs)
            arrived(vbuf, source, 1, j, mate_sem, theirs)
            attend(kbuf[source], vbuf[source], source * n_col * shard, False)

    for head in range(heads):
        inverse = 1.0 / total_ref[head : head + 1, :]
        result = (acc_ref[head] * inverse).T
        o_ref[:, head * HEAD_DIM : (head + 1) * HEAD_DIM] = result.astype(o_ref.dtype)

    @pl.loop(0, steps)
    def _(j):
        source = source_of(j)

        @pl.when(needs(row, source) | (j == 0))
        def _():
            for wanted, sends, recvs, at, device in relays(j, source, j % 2 == 0):

                @pl.when(wanted)
                def _():
                    for which, buf in enumerate((kbuf, vbuf)):
                        part = buf.at[source, mine, :]
                        send(part, buf, source, which, j, sends, recvs, at, device).wait_send()


def shards(n_row, n_col, queries, keys, values, doc_lengths):
    shard, width = queries.shape
    lanes = 2 if n_row % 2 == 0 else 1
    span = shard * n_row * n_col
    longest = (3 * span) // 4
    reach = min(n_row - 1, -(-longest // (shard * n_col)))
    levels = n_row // lanes
    steps = 2 * (min(levels - 1, (reach + lanes - 1) // lanes) + 1)
    tile = shard * n_col
    heads = width // HEAD_DIM
    vmem = pl.BlockSpec(memory_space=pltpu.VMEM)
    whole = pl.BlockSpec(memory_space=pltpu.HBM)
    sems = pltpu.SemaphoreType.DMA((2, steps))
    return pl.pallas_call(
        functools.partial(kernel, n_row, n_col, lanes, reach),
        out_shape=jax.ShapeDtypeStruct(queries.shape, queries.dtype),
        in_specs=[pl.BlockSpec(memory_space=pltpu.SMEM), whole, whole, whole],
        out_specs=vmem,
        scratch_shapes=[
            pltpu.VMEM((n_row, tile, HEAD_DIM), keys.dtype),
            pltpu.VMEM((n_row, tile, HEAD_DIM), values.dtype),
            pltpu.VMEM((heads, shard), jnp.float32),
            pltpu.VMEM((heads, shard), jnp.float32),
            pltpu.VMEM((heads, HEAD_DIM, shard), jnp.float32),
            pltpu.VMEM((heads, shard, 2 * HEAD_DIM), queries.dtype),
            pltpu.VMEM((2, tile, shard), jnp.float32),
            pltpu.SemaphoreType.DMA((2 + heads,)),
            sems,
            sems,
            sems,
            sems,
            sems,
        ],
        compiler_params=pltpu.CompilerParams(
            collective_id=0, has_side_effects=True, vmem_limit_bytes=24 << 20
        ),
        name="attend",
    )(doc_lengths, queries, keys, values)


def solution(mesh):
    placed = P(("groups", "row", "col"), None)
    return jax.shard_map(
        functools.partial(shards, mesh.shape["row"], mesh.shape["col"]),
        mesh=mesh,
        in_specs=(placed, placed, placed, P("groups")),
        out_specs=placed,
        check_vma=False,
    )
```

```python
import functools

import jax
import jax.numpy as jnp
from jax import lax
from jax.experimental import pallas as pl
from jax.experimental.pallas import tpu as pltpu
from jax.sharding import PartitionSpec as P

HEAD_DIM = 128
RATE = HEAD_DIM ** (-0.5) * 1.4426950408889634
MASKED = -1e30


def kernel(
    n_row,
    n_col,
    lanes,
    reach,
    lens_ref,
    q_ref,
    k_ref,
    v_ref,
    o_ref,
    kbuf,
    vbuf,
    top_ref,
    total_ref,
    acc_ref,
    qa_ref,
    s_ref,
    load_sem,
    in_sem,
    mate_sem,
    up_send,
    cross_send,
    mate_send,
):
    shard = q_ref.shape[0]
    heads = q_ref.shape[1] // HEAD_DIM
    levels = n_row // lanes
    steps = 2 * (min(levels - 1, (reach + lanes - 1) // lanes) + 1)
    row = lax.axis_index("row")
    col = lax.axis_index("col")
    level = row // lanes
    lane = row % lanes
    mate = 1 - col
    other = level * lanes + (lanes - 1 - lane)
    mine = pl.ds(pl.multiple_of(col * shard, shard), shard)
    theirs = pl.ds(pl.multiple_of(mate * shard, shard), shard)

    def needs(reader, source):
        return (source >= 0) & (reader > source) & (reader - source <= reach)

    has_up = level + 1 < levels
    has_down = level > 0
    has_other = lanes > 1

    barrier = pltpu.get_barrier_semaphore()
    pl.semaphore_signal(barrier, inc=1, device_id={"col": mate})
    if has_other:
        pl.semaphore_signal(barrier, inc=1, device_id={"row": other})

    @pl.when(has_up)
    def _():
        pl.semaphore_signal(barrier, inc=1, device_id={"row": row + lanes})

    @pl.when(has_down)
    def _():
        pl.semaphore_signal(barrier, inc=1, device_id={"row": row - lanes})

    loads = [
        pltpu.make_async_copy(k_ref, kbuf.at[row, mine, :], load_sem.at[0]),
        pltpu.make_async_copy(v_ref, vbuf.at[row, mine, :], load_sem.at[1]),
    ]
    for head in range(heads):
        part = q_ref.at[:, head * HEAD_DIM : (head + 1) * HEAD_DIM]
        loads.append(
            pltpu.make_async_copy(part, qa_ref.at[head, :, :HEAD_DIM], load_sem.at[2 + head])
        )
    for load in loads:
        load.start()

    count = 1 + int(has_other) + has_up.astype(jnp.int32) + has_down.astype(jnp.int32)
    pl.semaphore_wait(barrier, count)

    def send(src, buf, source, which, j, sends, recvs, at, device):
        return pltpu.make_async_remote_copy(
            src_ref=src,
            dst_ref=buf.at[source, mine, :],
            send_sem=sends.at[which, j],
            recv_sem=recvs.at[which, at],
            device_id=device,
            device_id_type=pl.DeviceIdType.MESH,
        )

    def source_of(j):
        dist, kind = j // 2, j % 2
        cross = kind == 1
        from_lane = jnp.where(cross, lanes - 1 - lane, lane)
        source = (level - dist) * lanes + from_lane
        if lanes == 1:
            source = jnp.where(cross, -1, source)
        return source

    def relays(j, source, straight):
        mate_wants = (source < row) | (col < mate)
        found = [(mate_wants, mate_send, mate_sem, j, {"col": mate})]
        up = straight & has_up & needs(row + lanes, source)
        found.append((up, up_send, in_sem, j + 2, {"row": row + lanes}))
        if has_other:
            cross = straight & needs(other, source)
            found.append((cross, cross_send, in_sem, j + 1, {"row": other}))
        return found

    def forward(src, buf, source, which, j, straight):
        for wanted, sends, recvs, at, device in reversed(relays(j, source, straight)):

            @pl.when(wanted)
            def _():
                send(src, buf, source, which, j, sends, recvs, at, device).start()

    def arrived(buf, source, which, j, sems, part):
        here = buf.at[source, part, :]
        pltpu.make_async_copy(here, here, sems.at[which, j]).wait()

    forward(k_ref, kbuf, row, 0, 0, True)
    forward(v_ref, vbuf, row, 1, 0, True)

    first = (row * n_col + col) * shard
    qpos = first + lax.broadcasted_iota(jnp.int32, (1, shard), 1)

    def within(places):
        return (places >= begins) & (places < ends)

    lanes_of = lax.broadcasted_iota(jnp.int32, (1, HEAD_DIM), 1)
    begins = jnp.zeros((1, HEAD_DIM), jnp.int32)
    ends = jnp.full((1, HEAD_DIM), n_row * n_col * shard, jnp.int32)
    end = jnp.int32(0)
    docs = lens_ref.shape[0]
    for doc in range(docs):
        begins = jnp.where(lanes_of == doc, end, begins)
        end = end + lens_ref[doc]
        ends = jnp.where(lanes_of == doc, end, ends)
    qplace = first + lax.broadcasted_iota(jnp.int32, (shard, HEAD_DIM), 0)
    member = jnp.where(within(qplace) & (lanes_of < docs), 1.0, 0.0).astype(jnp.bfloat16)
    for head in range(heads):
        qa_ref[head, :, HEAD_DIM:] = member
    for load in loads:
        load.wait()

    def attend(kblock, vblock, kfirst, fresh):
        count = kblock.shape[0]
        kplace = kfirst + lax.broadcasted_iota(jnp.int32, (count, HEAD_DIM), 0)
        apart = jnp.where(within(kplace), 0.0, MASKED).astype(jnp.bfloat16)
        kwide = jnp.concatenate([kblock, apart], axis=1)
        if fresh:
            kpos = kfirst + lax.broadcasted_iota(jnp.int32, (count, shard), 0)
            bias = jnp.where(kpos <= qpos, jnp.float32(0.0), jnp.float32(MASKED))
        vflip = vblock.T

        def score(head):
            scores = lax.dot_general(
                kwide, qa_ref[head], (((1,), (1,)), ((), ())), preferred_element_type=jnp.float32
            )
            if fresh:
                scores = scores + bias
            s_ref[head % 2, :count, :] = scores
            top = jnp.max(scores, axis=0, keepdims=True)
            if fresh:
                return top, top
            before = top_ref[head : head + 1, :]
            return before, jnp.maximum(before, top)

        ahead = score(0)
        for head in range(heads):
            before, top = ahead
            if head + 1 < heads:
                ahead = score(head + 1)
            weights = jnp.exp2((s_ref[head % 2, :count, :] - top) * RATE)
            total = jnp.sum(weights, axis=0, keepdims=True)
            summed = jnp.dot(
                vflip, weights.astype(jnp.bfloat16), preferred_element_type=jnp.float32
            )
            if not fresh:
                factor = jnp.exp2((before - top) * RATE)
                total = total + total_ref[head : head + 1, :] * factor
                summed = summed + acc_ref[head] * factor
            top_ref[head : head + 1, :] = top
            total_ref[head : head + 1, :] = total
            acc_ref[head] = summed

    attend(kbuf[row, mine, :], vbuf[row, mine, :], first, True)

    @pl.when(col > 0)
    def _():
        arrived(kbuf, row, 0, 0, mate_sem, theirs)
        arrived(vbuf, row, 1, 0, mate_sem, theirs)
        attend(kbuf[row, :shard, :], vbuf[row, :shard, :], row * n_col * shard, False)

    def relay(j):
        source = source_of(j)

        @pl.when((j < steps) & needs(row, source))
        def _():
            for which, buf in enumerate((kbuf, vbuf)):
                arrived(buf, source, which, j, in_sem, mine)
                forward(buf.at[source, mine, :], buf, source, which, j, j % 2 == 0)

    @pl.loop(1, steps)
    def _(j):
        relay(2 * j - 1)
        relay(2 * j)
        source = source_of(j)

        @pl.when(needs(row, source))
        def _():
            arrived(kbuf, source, 0, j, mate_sem, theirs)
            arrived(vbuf, source, 1, j, mate_sem, theirs)
            attend(kbuf[source], vbuf[source], source * n_col * shard, False)

    for head in range(heads):
        inverse = 1.0 / total_ref[head : head + 1, :]
        result = (acc_ref[head] * inverse).T
        o_ref[:, head * HEAD_DIM : (head + 1) * HEAD_DIM] = result.astype(o_ref.dtype)

    @pl.loop(0, steps)
    def _(j):
        source = source_of(j)

        @pl.when(needs(row, source) | (j == 0))
        def _():
            for wanted, sends, recvs, at, device in relays(j, source, j % 2 == 0):

                @pl.when(wanted)
                def _():
                    for which, buf in enumerate((kbuf, vbuf)):
                        part = buf.at[source, mine, :]
                        send(part, buf, source, which, j, sends, recvs, at, device).wait_send()


def shards(n_row, n_col, queries, keys, values, doc_lengths):
    shard, width = queries.shape
    lanes = 2 if n_row % 2 == 0 else 1
    span = shard * n_row * n_col
    longest = (3 * span) // 4
    reach = min(n_row - 1, -(-longest // (shard * n_col)))
    levels = n_row // lanes
    steps = 2 * (min(levels - 1, (reach + lanes - 1) // lanes) + 1)
    tile = shard * n_col
    heads = width // HEAD_DIM
    vmem = pl.BlockSpec(memory_space=pltpu.VMEM)
    whole = pl.BlockSpec(memory_space=pltpu.HBM)
    sems = pltpu.SemaphoreType.DMA((2, steps))
    return pl.pallas_call(
        functools.partial(kernel, n_row, n_col, lanes, reach),
        out_shape=jax.ShapeDtypeStruct(queries.shape, queries.dtype),
        in_specs=[pl.BlockSpec(memory_space=pltpu.SMEM), whole, whole, whole],
        out_specs=vmem,
        scratch_shapes=[
            pltpu.VMEM((n_row, tile, HEAD_DIM), keys.dtype),
            pltpu.VMEM((n_row, tile, HEAD_DIM), values.dtype),
            pltpu.VMEM((heads, shard), jnp.float32),
            pltpu.VMEM((heads, shard), jnp.float32),
            pltpu.VMEM((heads, HEAD_DIM, shard), jnp.float32),
            pltpu.VMEM((heads, shard, 2 * HEAD_DIM), queries.dtype),
            pltpu.VMEM((2, tile, shard), jnp.float32),
            pltpu.SemaphoreType.DMA((2 + heads,)),
            sems,
            sems,
            sems,
            sems,
            sems,
        ],
        compiler_params=pltpu.CompilerParams(
            collective_id=0, has_side_effects=True, vmem_limit_bytes=60 << 20
        ),
        name="attend",
    )(doc_lengths, queries, keys, values)


def solution(mesh):
    placed = P(("groups", "row", "col"), None)
    return jax.shard_map(
        functools.partial(shards, mesh.shape["row"], mesh.shape["col"]),
        mesh=mesh,
        in_specs=(placed, placed, placed, P("groups")),
        out_specs=placed,
        check_vma=False,
    )
```

```python
import functools

import jax
import jax.numpy as jnp
from jax import lax
from jax.experimental import pallas as pl
from jax.experimental.pallas import tpu as pltpu
from jax.sharding import PartitionSpec as P

HEAD_DIM = 128
RATE = HEAD_DIM ** (-0.5) * 1.4426950408889634
MASKED = -1e30
AHEAD_SLOTS = 8


def kernel(
    n_row,
    n_col,
    lanes,
    reach,
    lens_ref,
    q_ref,
    k_ref,
    v_ref,
    o_ref,
    kbuf,
    vbuf,
    top_ref,
    total_ref,
    acc_ref,
    qa_ref,
    s_ref,
    load_sem,
    in_sem,
    mate_sem,
    up_send,
    cross_send,
    mate_send,
):
    shard = q_ref.shape[0]
    heads = q_ref.shape[1] // HEAD_DIM
    levels = n_row // lanes
    steps = 2 * (min(levels - 1, (reach + lanes - 1) // lanes) + 1)
    row = lax.axis_index("row")
    col = lax.axis_index("col")
    level = row // lanes
    lane = row % lanes
    mate = 1 - col
    other = level * lanes + (lanes - 1 - lane)
    mine = pl.ds(pl.multiple_of(col * shard, shard), shard)
    theirs = pl.ds(pl.multiple_of(mate * shard, shard), shard)

    def needs(reader, source):
        return (source >= 0) & (reader > source) & (reader - source <= reach)

    has_up = level + 1 < levels
    has_down = level > 0
    has_other = lanes > 1

    barrier = pltpu.get_barrier_semaphore()
    pl.semaphore_signal(barrier, inc=1, device_id={"col": mate})
    if has_other:
        pl.semaphore_signal(barrier, inc=1, device_id={"row": other})

    @pl.when(has_up)
    def _():
        pl.semaphore_signal(barrier, inc=1, device_id={"row": row + lanes})

    @pl.when(has_down)
    def _():
        pl.semaphore_signal(barrier, inc=1, device_id={"row": row - lanes})

    loads = [
        pltpu.make_async_copy(k_ref, kbuf.at[row, mine, :], load_sem.at[0]),
        pltpu.make_async_copy(v_ref, vbuf.at[row, mine, :], load_sem.at[1]),
    ]
    for head in range(heads):
        part = q_ref.at[:, head * HEAD_DIM : (head + 1) * HEAD_DIM]
        loads.append(
            pltpu.make_async_copy(part, qa_ref.at[head, :, :HEAD_DIM], load_sem.at[2 + head])
        )
    for load in loads:
        load.start()

    count = 1 + int(has_other) + has_up.astype(jnp.int32) + has_down.astype(jnp.int32)
    pl.semaphore_wait(barrier, count)

    def send(src, buf, source, which, j, sends, recvs, at, device):
        return pltpu.make_async_remote_copy(
            src_ref=src,
            dst_ref=buf.at[source, mine, :],
            send_sem=sends.at[which, j],
            recv_sem=recvs.at[which, at],
            device_id=device,
            device_id_type=pl.DeviceIdType.MESH,
        )

    def source_of(j):
        dist, kind = j // 2, j % 2
        cross = kind == 1
        from_lane = jnp.where(cross, lanes - 1 - lane, lane)
        source = (level - dist) * lanes + from_lane
        if lanes == 1:
            source = jnp.where(cross, -1, source)
        return source

    def relays(j, source, straight):
        mate_wants = (source < row) | (col < mate)
        found = [(mate_wants, mate_send, mate_sem, j, {"col": mate})]
        up = straight & has_up & needs(row + lanes, source)
        found.append((up, up_send, in_sem, j + 2, {"row": row + lanes}))
        if has_other:
            cross = straight & needs(other, source)
            found.append((cross, cross_send, in_sem, j + 1, {"row": other}))
        return found

    def forward(src, buf, source, which, j, straight):
        for wanted, sends, recvs, at, device in reversed(relays(j, source, straight)):

            @pl.when(wanted)
            def _():
                send(src, buf, source, which, j, sends, recvs, at, device).start()

    def arrived(buf, source, which, j, sems, part):
        here = buf.at[source, part, :]
        pltpu.make_async_copy(here, here, sems.at[which, j]).wait()

    forward(k_ref, kbuf, row, 0, 0, True)
    forward(v_ref, vbuf, row, 1, 0, True)

    first = (row * n_col + col) * shard
    qpos = first + lax.broadcasted_iota(jnp.int32, (1, shard), 1)

    def within(places):
        return (places >= begins) & (places < ends)

    lanes_of = lax.broadcasted_iota(jnp.int32, (1, HEAD_DIM), 1)
    begins = jnp.zeros((1, HEAD_DIM), jnp.int32)
    ends = jnp.full((1, HEAD_DIM), n_row * n_col * shard, jnp.int32)
    end = jnp.int32(0)
    docs = lens_ref.shape[0]
    for doc in range(docs):
        begins = jnp.where(lanes_of == doc, end, begins)
        end = end + lens_ref[doc]
        ends = jnp.where(lanes_of == doc, end, ends)
    qplace = first + lax.broadcasted_iota(jnp.int32, (shard, HEAD_DIM), 0)
    member = jnp.where(within(qplace) & (lanes_of < docs), 1.0, 0.0).astype(jnp.bfloat16)
    for head in range(heads):
        qa_ref[head, :, HEAD_DIM:] = member
    for load in loads:
        load.wait()

    def attend(kblock, vblock, kfirst, fresh):
        count = kblock.shape[0]
        kplace = kfirst + lax.broadcasted_iota(jnp.int32, (count, HEAD_DIM), 0)
        apart = jnp.where(within(kplace), 0.0, MASKED).astype(jnp.bfloat16)
        kwide = jnp.concatenate([kblock, apart], axis=1)
        if fresh:
            kpos = kfirst + lax.broadcasted_iota(jnp.int32, (count, shard), 0)
            bias = jnp.where(kpos <= qpos, jnp.float32(0.0), jnp.float32(MASKED))
        vflip = vblock.T

        def score(head):
            scores = lax.dot_general(
                kwide, qa_ref[head], (((1,), (1,)), ((), ())), preferred_element_type=jnp.float32
            )
            if fresh:
                scores = scores + bias
            s_ref[head % AHEAD_SLOTS, :count, :] = scores
            top = jnp.max(scores, axis=0, keepdims=True)
            if fresh:
                return top, top
            before = top_ref[head : head + 1, :]
            return before, jnp.maximum(before, top)

        tops = [score(head) for head in range(AHEAD_SLOTS - 1)]
        for head in range(heads):
            before, top = tops[head]
            if head + AHEAD_SLOTS - 1 < heads:
                tops.append(score(head + AHEAD_SLOTS - 1))
            weights = jnp.exp2((s_ref[head % AHEAD_SLOTS, :count, :] - top) * RATE)
            total = jnp.sum(weights, axis=0, keepdims=True)
            summed = jnp.dot(
                vflip, weights.astype(jnp.bfloat16), preferred_element_type=jnp.float32
            )
            if not fresh:
                factor = jnp.exp2((before - top) * RATE)
                total = total + total_ref[head : head + 1, :] * factor
                summed = summed + acc_ref[head] * factor
            top_ref[head : head + 1, :] = top
            total_ref[head : head + 1, :] = total
            acc_ref[head] = summed

    attend(kbuf[row, mine, :], vbuf[row, mine, :], first, True)

    def relay(j):
        source = source_of(j)

        @pl.when((j < steps) & needs(row, source))
        def _():
            for which, buf in enumerate((kbuf, vbuf)):
                arrived(buf, source, which, j, in_sem, mine)
                forward(buf.at[source, mine, :], buf, source, which, j, j % 2 == 0)

    relay(1)
    relay(2)

    @pl.when(col > 0)
    def _():
        arrived(kbuf, row, 0, 0, mate_sem, theirs)
        arrived(vbuf, row, 1, 0, mate_sem, theirs)
        attend(kbuf[row, :shard, :], vbuf[row, :shard, :], row * n_col * shard, False)

    @pl.loop(1, steps)
    def _(j):
        source = source_of(j)

        @pl.when(needs(row, source))
        def _():
            arrived(kbuf, source, 0, j, mate_sem, theirs)
            arrived(vbuf, source, 1, j, mate_sem, theirs)
            attend(kbuf[source], vbuf[source], source * n_col * shard, False)

        relay(2 * j + 1)
        relay(2 * j + 2)

    for head in range(heads):
        inverse = 1.0 / total_ref[head : head + 1, :]
        result = (acc_ref[head] * inverse).T
        o_ref[:, head * HEAD_DIM : (head + 1) * HEAD_DIM] = result.astype(o_ref.dtype)

    @pl.loop(0, steps)
    def _(j):
        source = source_of(j)

        @pl.when(needs(row, source) | (j == 0))
        def _():
            for wanted, sends, recvs, at, device in relays(j, source, j % 2 == 0):

                @pl.when(wanted)
                def _():
                    for which, buf in enumerate((kbuf, vbuf)):
                        part = buf.at[source, mine, :]
                        send(part, buf, source, which, j, sends, recvs, at, device).wait_send()


def shards(n_row, n_col, queries, keys, values, doc_lengths):
    shard, width = queries.shape
    lanes = 2 if n_row % 2 == 0 else 1
    span = shard * n_row * n_col
    longest = (3 * span) // 4
    reach = min(n_row - 1, -(-longest // (shard * n_col)))
    levels = n_row // lanes
    steps = 2 * (min(levels - 1, (reach + lanes - 1) // lanes) + 1)
    tile = shard * n_col
    heads = width // HEAD_DIM
    vmem = pl.BlockSpec(memory_space=pltpu.VMEM)
    whole = pl.BlockSpec(memory_space=pltpu.HBM)
    sems = pltpu.SemaphoreType.DMA((2, steps))
    return pl.pallas_call(
        functools.partial(kernel, n_row, n_col, lanes, reach),
        out_shape=jax.ShapeDtypeStruct(queries.shape, queries.dtype),
        in_specs=[pl.BlockSpec(memory_space=pltpu.SMEM), whole, whole, whole],
        out_specs=vmem,
        scratch_shapes=[
            pltpu.VMEM((n_row, tile, HEAD_DIM), keys.dtype),
            pltpu.VMEM((n_row, tile, HEAD_DIM), values.dtype),
            pltpu.VMEM((heads, shard), jnp.float32),
            pltpu.VMEM((heads, shard), jnp.float32),
            pltpu.VMEM((heads, HEAD_DIM, shard), jnp.float32),
            pltpu.VMEM((heads, shard, 2 * HEAD_DIM), queries.dtype),
            pltpu.VMEM((AHEAD_SLOTS, tile, shard), jnp.float32),
            pltpu.SemaphoreType.DMA((2 + heads,)),
            sems,
            sems,
            sems,
            sems,
            sems,
        ],
        compiler_params=pltpu.CompilerParams(
            collective_id=0, has_side_effects=True, vmem_limit_bytes=60 << 20
        ),
        name="attend",
    )(doc_lengths, queries, keys, values)


def solution(mesh):
    placed = P(("groups", "row", "col"), None)
    return jax.shard_map(
        functools.partial(shards, mesh.shape["row"], mesh.shape["col"]),
        mesh=mesh,
        in_specs=(placed, placed, placed, P("groups")),
        out_specs=placed,
        check_vma=False,
    )
```

```python
import functools

import jax
import jax.numpy as jnp
from jax import lax
from jax.experimental import pallas as pl
from jax.experimental.pallas import tpu as pltpu
from jax.sharding import PartitionSpec as P

HEAD_DIM = 128
RATE = HEAD_DIM ** (-0.5) * 1.4426950408889634
MASKED = -1e30
AHEAD_SLOTS = 8


def kernel(
    n_row,
    n_col,
    lanes,
    reach,
    lens_ref,
    q_ref,
    k_ref,
    v_ref,
    o_ref,
    kbuf,
    vbuf,
    top_ref,
    total_ref,
    acc_ref,
    qa_ref,
    s_ref,
    load_sem,
    in_sem,
    mate_sem,
    up_send,
    cross_send,
    mate_send,
):
    shard = q_ref.shape[0]
    heads = q_ref.shape[1] // HEAD_DIM
    levels = n_row // lanes
    steps = 2 * (min(levels - 1, (reach + lanes - 1) // lanes) + 1)
    row = lax.axis_index("row")
    col = lax.axis_index("col")
    level = row // lanes
    lane = row % lanes
    mate = 1 - col
    other = level * lanes + (lanes - 1 - lane)
    mine = pl.ds(pl.multiple_of(col * shard, shard), shard)
    theirs = pl.ds(pl.multiple_of(mate * shard, shard), shard)

    def needs(reader, source):
        return (source >= 0) & (reader > source) & (reader - source <= reach)

    has_up = level + 1 < levels
    has_down = level > 0
    has_other = lanes > 1

    barrier = pltpu.get_barrier_semaphore()
    pl.semaphore_signal(barrier, inc=1, device_id={"col": mate})
    if has_other:
        pl.semaphore_signal(barrier, inc=1, device_id={"row": other})

    @pl.when(has_up)
    def _():
        pl.semaphore_signal(barrier, inc=1, device_id={"row": row + lanes})

    @pl.when(has_down)
    def _():
        pl.semaphore_signal(barrier, inc=1, device_id={"row": row - lanes})

    loads = [
        pltpu.make_async_copy(k_ref, kbuf.at[row, mine, :], load_sem.at[0]),
        pltpu.make_async_copy(v_ref, vbuf.at[row, mine, :], load_sem.at[1]),
    ]
    for head in range(heads):
        part = q_ref.at[:, head * HEAD_DIM : (head + 1) * HEAD_DIM]
        loads.append(
            pltpu.make_async_copy(part, qa_ref.at[head, :, :HEAD_DIM], load_sem.at[2 + head])
        )
    for load in loads:
        load.start()

    count = 1 + int(has_other) + has_up.astype(jnp.int32) + has_down.astype(jnp.int32)
    pl.semaphore_wait(barrier, count)

    def send(src, buf, source, which, j, sends, recvs, at, device):
        return pltpu.make_async_remote_copy(
            src_ref=src,
            dst_ref=buf.at[source, mine, :],
            send_sem=sends.at[which, j],
            recv_sem=recvs.at[which, at],
            device_id=device,
            device_id_type=pl.DeviceIdType.MESH,
        )

    def source_of(j):
        dist, kind = j // 2, j % 2
        cross = kind == 1
        from_lane = jnp.where(cross, lanes - 1 - lane, lane)
        source = (level - dist) * lanes + from_lane
        if lanes == 1:
            source = jnp.where(cross, -1, source)
        return source

    def relays(j, source, straight):
        mate_wants = (source < row) | (col < mate)
        found = [(mate_wants, mate_send, mate_sem, j, {"col": mate})]
        up = straight & has_up & needs(row + lanes, source)
        found.append((up, up_send, in_sem, j + 2, {"row": row + lanes}))
        if has_other:
            cross = straight & needs(other, source)
            found.append((cross, cross_send, in_sem, j + 1, {"row": other}))
        return found

    def forward(src, buf, source, which, j, straight):
        for wanted, sends, recvs, at, device in reversed(relays(j, source, straight)):

            @pl.when(wanted)
            def _():
                send(src, buf, source, which, j, sends, recvs, at, device).start()

    def arrived(buf, source, which, j, sems, part):
        here = buf.at[source, part, :]
        pltpu.make_async_copy(here, here, sems.at[which, j]).wait()

    forward(k_ref, kbuf, row, 0, 0, True)
    forward(v_ref, vbuf, row, 1, 0, True)

    first = (row * n_col + col) * shard
    qpos = first + lax.broadcasted_iota(jnp.int32, (1, shard), 1)

    def within(places):
        return (places >= begins) & (places < ends)

    lanes_of = lax.broadcasted_iota(jnp.int32, (1, HEAD_DIM), 1)
    begins = jnp.zeros((1, HEAD_DIM), jnp.int32)
    ends = jnp.full((1, HEAD_DIM), n_row * n_col * shard, jnp.int32)
    end = jnp.int32(0)
    docs = lens_ref.shape[0]
    for doc in range(docs):
        begins = jnp.where(lanes_of == doc, end, begins)
        end = end + lens_ref[doc]
        ends = jnp.where(lanes_of == doc, end, ends)
    qplace = first + lax.broadcasted_iota(jnp.int32, (shard, HEAD_DIM), 0)
    member = jnp.where(within(qplace) & (lanes_of < docs), 1.0, 0.0).astype(jnp.bfloat16)
    for head in range(heads):
        qa_ref[head, :, HEAD_DIM:] = member
    for load in loads:
        load.wait()

    def attend(kblock, vblock, kfirst, fresh):
        count = kblock.shape[0]
        kplace = kfirst + lax.broadcasted_iota(jnp.int32, (count, HEAD_DIM), 0)
        apart = jnp.where(within(kplace), 0.0, MASKED).astype(jnp.bfloat16)
        kwide = jnp.concatenate([kblock, apart], axis=1)
        if fresh:
            kpos = kfirst + lax.broadcasted_iota(jnp.int32, (count, shard), 0)
            bias = jnp.where(kpos <= qpos, jnp.float32(0.0), jnp.float32(MASKED))
        vflip = vblock.T

        def score(head):
            scores = lax.dot_general(
                kwide, qa_ref[head], (((1,), (1,)), ((), ())), preferred_element_type=jnp.float32
            )
            if fresh:
                scores = scores + bias
            s_ref[head % AHEAD_SLOTS, :count, :] = scores
            top = jnp.max(scores, axis=0, keepdims=True)
            if fresh:
                return top, top
            before = top_ref[head : head + 1, :]
            return before, jnp.maximum(before, top)

        tops = [score(head) for head in range(AHEAD_SLOTS - 1)]
        for head in range(heads):
            before, top = tops[head]
            if head + AHEAD_SLOTS - 1 < heads:
                tops.append(score(head + AHEAD_SLOTS - 1))
            weights = jnp.exp2((s_ref[head % AHEAD_SLOTS, :count, :] - top) * RATE)
            total = jnp.sum(weights, axis=0, keepdims=True)
            summed = jnp.dot(
                vflip, weights.astype(jnp.bfloat16), preferred_element_type=jnp.float32
            )
            if not fresh:
                factor = jnp.exp2((before - top) * RATE)
                total = total + total_ref[head : head + 1, :] * factor
                summed = summed + acc_ref[head] * factor
            top_ref[head : head + 1, :] = top
            total_ref[head : head + 1, :] = total
            acc_ref[head] = summed

    attend(kbuf[row, mine, :], vbuf[row, mine, :], first, True)

    def relay(j, least):
        source = source_of(j)

        @pl.when((j >= least) & (j < steps) & needs(row, source))
        def _():
            for which, buf in enumerate((kbuf, vbuf)):
                arrived(buf, source, which, j, in_sem, mine)
                forward(buf.at[source, mine, :], buf, source, which, j, j % 2 == 0)

    relay(jnp.int32(1), 1)
    relay(jnp.int32(2), 1)

    @pl.when(col > 0)
    def _():
        arrived(kbuf, row, 0, 0, mate_sem, theirs)
        arrived(vbuf, row, 1, 0, mate_sem, theirs)
        attend(kbuf[row, :shard, :], vbuf[row, :shard, :], row * n_col * shard, False)

    @pl.loop(1, steps)
    def _(j):
        source = source_of(j)

        @pl.when(needs(row, source))
        def _():
            arrived(kbuf, source, 0, j, mate_sem, theirs)
            arrived(vbuf, source, 1, j, mate_sem, theirs)
            attend(kbuf[source], vbuf[source], source * n_col * shard, False)

        ahead = 2 * (j - jnp.where(lane == lanes - 1, 0, 1)) + 1
        relay(ahead, 3)
        relay(ahead + 1, 3)

    for head in range(heads):
        inverse = 1.0 / total_ref[head : head + 1, :]
        result = (acc_ref[head] * inverse).T
        o_ref[:, head * HEAD_DIM : (head + 1) * HEAD_DIM] = result.astype(o_ref.dtype)

    @pl.loop(0, steps)
    def _(j):
        source = source_of(j)

        @pl.when(needs(row, source) | (j == 0))
        def _():
            for wanted, sends, recvs, at, device in relays(j, source, j % 2 == 0):

                @pl.when(wanted)
                def _():
                    for which, buf in enumerate((kbuf, vbuf)):
                        part = buf.at[source, mine, :]
                        send(part, buf, source, which, j, sends, recvs, at, device).wait_send()


def shards(n_row, n_col, queries, keys, values, doc_lengths):
    shard, width = queries.shape
    lanes = 2 if n_row % 2 == 0 else 1
    span = shard * n_row * n_col
    longest = (3 * span) // 4
    reach = min(n_row - 1, -(-longest // (shard * n_col)))
    levels = n_row // lanes
    steps = 2 * (min(levels - 1, (reach + lanes - 1) // lanes) + 1)
    tile = shard * n_col
    heads = width // HEAD_DIM
    vmem = pl.BlockSpec(memory_space=pltpu.VMEM)
    whole = pl.BlockSpec(memory_space=pltpu.HBM)
    sems = pltpu.SemaphoreType.DMA((2, steps))
    return pl.pallas_call(
        functools.partial(kernel, n_row, n_col, lanes, reach),
        out_shape=jax.ShapeDtypeStruct(queries.shape, queries.dtype),
        in_specs=[pl.BlockSpec(memory_space=pltpu.SMEM), whole, whole, whole],
        out_specs=vmem,
        scratch_shapes=[
            pltpu.VMEM((n_row, tile, HEAD_DIM), keys.dtype),
            pltpu.VMEM((n_row, tile, HEAD_DIM), values.dtype),
            pltpu.VMEM((heads, shard), jnp.float32),
            pltpu.VMEM((heads, shard), jnp.float32),
            pltpu.VMEM((heads, HEAD_DIM, shard), jnp.float32),
            pltpu.VMEM((heads, shard, 2 * HEAD_DIM), queries.dtype),
            pltpu.VMEM((AHEAD_SLOTS, tile, shard), jnp.float32),
            pltpu.SemaphoreType.DMA((2 + heads,)),
            sems,
            sems,
            sems,
            sems,
            sems,
        ],
        compiler_params=pltpu.CompilerParams(
            collective_id=0, has_side_effects=True, vmem_limit_bytes=24 << 20
        ),
        name="attend",
    )(*(pltpu.with_memory_space_constraint(x, pltpu.HBM) for x in (doc_lengths, queries, keys, values)))


def solution(mesh):
    placed = P(("groups", "row", "col"), None)
    return jax.shard_map(
        functools.partial(shards, mesh.shape["row"], mesh.shape["col"]),
        mesh=mesh,
        in_specs=(placed, placed, placed, P("groups")),
        out_specs=placed,
        check_vma=False,
    )
```

```python
import functools

import jax
import jax.numpy as jnp
from jax import lax
from jax.experimental import pallas as pl
from jax.experimental.pallas import tpu as pltpu
from jax.sharding import PartitionSpec as P

HEAD_DIM = 128
RATE = HEAD_DIM ** (-0.5) * 1.4426950408889634
MASKED = -1e30
AHEAD_SLOTS = 8


def kernel(
    n_row,
    n_col,
    lanes,
    reach,
    lens_ref,
    q_ref,
    k_ref,
    v_ref,
    o_ref,
    kbuf,
    vbuf,
    top_ref,
    total_ref,
    acc_ref,
    qa_ref,
    s_ref,
    load_sem,
    in_sem,
    mate_sem,
    up_send,
    cross_send,
    mate_send,
):
    shard = q_ref.shape[0]
    heads = q_ref.shape[1] // HEAD_DIM
    levels = n_row // lanes
    steps = 2 * (min(levels - 1, (reach + lanes - 1) // lanes) + 1)
    row = lax.axis_index("row")
    col = lax.axis_index("col")
    level = row // lanes
    lane = row % lanes
    mate = 1 - col
    other = level * lanes + (lanes - 1 - lane)
    mine = pl.ds(pl.multiple_of(col * shard, shard), shard)
    theirs = pl.ds(pl.multiple_of(mate * shard, shard), shard)

    def needs(reader, source):
        return (source >= 0) & (reader > source) & (reader - source <= reach)

    has_up = level + 1 < levels
    has_down = level > 0
    has_other = lanes > 1

    barrier = pltpu.get_barrier_semaphore()
    pl.semaphore_signal(barrier, inc=1, device_id={"col": mate})
    if has_other:
        pl.semaphore_signal(barrier, inc=1, device_id={"row": other})

    @pl.when(has_up)
    def _():
        pl.semaphore_signal(barrier, inc=1, device_id={"row": row + lanes})

    @pl.when(has_down)
    def _():
        pl.semaphore_signal(barrier, inc=1, device_id={"row": row - lanes})

    loads = [
        pltpu.make_async_copy(k_ref, kbuf.at[row, mine, :], load_sem.at[0]),
        pltpu.make_async_copy(v_ref, vbuf.at[row, mine, :], load_sem.at[1]),
    ]
    for head in range(heads):
        part = q_ref.at[:, head * HEAD_DIM : (head + 1) * HEAD_DIM]
        loads.append(
            pltpu.make_async_copy(part, qa_ref.at[head, :, :HEAD_DIM], load_sem.at[2 + head])
        )
    for load in loads:
        load.start()

    count = 1 + int(has_other) + has_up.astype(jnp.int32) + has_down.astype(jnp.int32)
    pl.semaphore_wait(barrier, count)

    def send(src, buf, source, which, j, sends, recvs, at, device):
        return pltpu.make_async_remote_copy(
            src_ref=src,
            dst_ref=buf.at[source, mine, :],
            send_sem=sends.at[which, j],
            recv_sem=recvs.at[which, at],
            device_id=device,
            device_id_type=pl.DeviceIdType.MESH,
        )

    def source_of(j):
        dist, kind = j // 2, j % 2
        cross = kind == 1
        from_lane = jnp.where(cross, lanes - 1 - lane, lane)
        source = (level - dist) * lanes + from_lane
        if lanes == 1:
            source = jnp.where(cross, -1, source)
        return source

    def relays(j, source, straight):
        mate_wants = (source < row) | (col < mate)
        found = [(mate_wants, mate_send, mate_sem, j, {"col": mate})]
        up = straight & has_up & needs(row + lanes, source)
        found.append((up, up_send, in_sem, j + 2, {"row": row + lanes}))
        if has_other:
            cross = straight & needs(other, source)
            found.append((cross, cross_send, in_sem, j + 1, {"row": other}))
        return found

    def forward(src, buf, source, which, j, straight):
        for wanted, sends, recvs, at, device in reversed(relays(j, source, straight)):

            @pl.when(wanted)
            def _():
                send(src, buf, source, which, j, sends, recvs, at, device).start()

    def arrived(buf, source, which, j, sems, part):
        here = buf.at[source, part, :]
        pltpu.make_async_copy(here, here, sems.at[which, j]).wait()

    forward(k_ref, kbuf, row, 0, 0, True)
    forward(v_ref, vbuf, row, 1, 0, True)

    first = (row * n_col + col) * shard
    qpos = first + lax.broadcasted_iota(jnp.int32, (1, shard), 1)

    def within(places):
        return (places >= begins) & (places < ends)

    lanes_of = lax.broadcasted_iota(jnp.int32, (1, HEAD_DIM), 1)
    begins = jnp.zeros((1, HEAD_DIM), jnp.int32)
    ends = jnp.full((1, HEAD_DIM), n_row * n_col * shard, jnp.int32)
    end = jnp.int32(0)
    docs = lens_ref.shape[0]
    for doc in range(docs):
        begins = jnp.where(lanes_of == doc, end, begins)
        end = end + lens_ref[doc]
        ends = jnp.where(lanes_of == doc, end, ends)
    qplace = first + lax.broadcasted_iota(jnp.int32, (shard, HEAD_DIM), 0)
    member = jnp.where(within(qplace) & (lanes_of < docs), 1.0, 0.0).astype(jnp.bfloat16)
    for head in range(heads):
        qa_ref[head, :, HEAD_DIM:] = member
    for load in loads:
        load.wait()

    def attend(kblock, vblock, kfirst, fresh):
        count = kblock.shape[0]
        kplace = kfirst + lax.broadcasted_iota(jnp.int32, (count, HEAD_DIM), 0)
        apart = jnp.where(within(kplace), 0.0, MASKED).astype(jnp.bfloat16)
        kwide = jnp.concatenate([kblock, apart], axis=1)
        if fresh:
            kpos = kfirst + lax.broadcasted_iota(jnp.int32, (count, shard), 0)
            bias = jnp.where(kpos <= qpos, jnp.float32(0.0), jnp.float32(MASKED))
        vflip = vblock.T

        def score(head):
            scores = lax.dot_general(
                kwide, qa_ref[head], (((1,), (1,)), ((), ())), preferred_element_type=jnp.float32
            )
            if fresh:
                scores = scores + bias
            s_ref[head % AHEAD_SLOTS, :count, :] = scores
            top = jnp.max(scores, axis=0, keepdims=True)
            if fresh:
                return top, top
            before = top_ref[head : head + 1, :]
            return before, jnp.maximum(before, top)

        tops = [score(head) for head in range(AHEAD_SLOTS - 1)]
        for head in range(heads):
            before, top = tops[head]
            if head + AHEAD_SLOTS - 1 < heads:
                tops.append(score(head + AHEAD_SLOTS - 1))
            weights = jnp.exp2((s_ref[head % AHEAD_SLOTS, :count, :] - top) * RATE)
            total = jnp.sum(weights, axis=0, keepdims=True)
            summed = jnp.dot(
                vflip, weights.astype(jnp.bfloat16), preferred_element_type=jnp.float32
            )
            if not fresh:
                factor = jnp.exp2((before - top) * RATE)
                total = total + total_ref[head : head + 1, :] * factor
                summed = summed + acc_ref[head] * factor
            top_ref[head : head + 1, :] = top
            total_ref[head : head + 1, :] = total
            acc_ref[head] = summed

    attend(kbuf[row, mine, :], vbuf[row, mine, :], first, True)

    def relay(j, least):
        source = source_of(j)

        @pl.when((j >= least) & (j < steps) & needs(row, source))
        def _():
            for which, buf in enumerate((kbuf, vbuf)):
                arrived(buf, source, which, j, in_sem, mine)
                forward(buf.at[source, mine, :], buf, source, which, j, j % 2 == 0)

    relay(jnp.int32(1), 1)
    relay(jnp.int32(2), 1)

    @pl.when(col > 0)
    def _():
        arrived(kbuf, row, 0, 0, mate_sem, theirs)
        arrived(vbuf, row, 1, 0, mate_sem, theirs)
        attend(kbuf[row, :shard, :], vbuf[row, :shard, :], row * n_col * shard, False)

    @pl.loop(1, steps)
    def _(j):
        source = source_of(j)

        @pl.when(needs(row, source))
        def _():
            arrived(kbuf, source, 0, j, mate_sem, theirs)
            arrived(vbuf, source, 1, j, mate_sem, theirs)
            attend(kbuf[source], vbuf[source], source * n_col * shard, False)

        ahead = 2 * (j - jnp.where(lane == lanes - 1, 0, 1)) + 1
        relay(ahead + 1, 3)
        relay(ahead, 3)

    for head in range(heads):
        inverse = 1.0 / total_ref[head : head + 1, :]
        result = (acc_ref[head] * inverse).T
        o_ref[:, head * HEAD_DIM : (head + 1) * HEAD_DIM] = result.astype(o_ref.dtype)

    @pl.loop(0, steps)
    def _(j):
        source = source_of(j)

        @pl.when(needs(row, source) | (j == 0))
        def _():
            for wanted, sends, recvs, at, device in relays(j, source, j % 2 == 0):

                @pl.when(wanted)
                def _():
                    for which, buf in enumerate((kbuf, vbuf)):
                        part = buf.at[source, mine, :]
                        send(part, buf, source, which, j, sends, recvs, at, device).wait_send()


def shards(n_row, n_col, queries, keys, values, doc_lengths):
    shard, width = queries.shape
    lanes = 2 if n_row % 2 == 0 else 1
    span = shard * n_row * n_col
    longest = (3 * span) // 4
    reach = min(n_row - 1, -(-longest // (shard * n_col)))
    levels = n_row // lanes
    steps = 2 * (min(levels - 1, (reach + lanes - 1) // lanes) + 1)
    tile = shard * n_col
    heads = width // HEAD_DIM
    vmem = pl.BlockSpec(memory_space=pltpu.VMEM)
    whole = pl.BlockSpec(memory_space=pltpu.HBM)
    sems = pltpu.SemaphoreType.DMA((2, steps))
    return pl.pallas_call(
        functools.partial(kernel, n_row, n_col, lanes, reach),
        out_shape=jax.ShapeDtypeStruct(queries.shape, queries.dtype),
        in_specs=[pl.BlockSpec(memory_space=pltpu.SMEM), whole, whole, whole],
        out_specs=vmem,
        scratch_shapes=[
            pltpu.VMEM((n_row, tile, HEAD_DIM), keys.dtype),
            pltpu.VMEM((n_row, tile, HEAD_DIM), values.dtype),
            pltpu.VMEM((heads, shard), jnp.float32),
            pltpu.VMEM((heads, shard), jnp.float32),
            pltpu.VMEM((heads, HEAD_DIM, shard), jnp.float32),
            pltpu.VMEM((heads, shard, 2 * HEAD_DIM), queries.dtype),
            pltpu.VMEM((AHEAD_SLOTS, tile, shard), jnp.float32),
            pltpu.SemaphoreType.DMA((2 + heads,)),
            sems,
            sems,
            sems,
            sems,
            sems,
        ],
        compiler_params=pltpu.CompilerParams(
            collective_id=0, has_side_effects=True, vmem_limit_bytes=24 << 20
        ),
        name="attend",
    )(*(pltpu.with_memory_space_constraint(x, pltpu.HBM) for x in (doc_lengths, queries, keys, values)))


def solution(mesh):
    placed = P(("groups", "row", "col"), None)
    return jax.shard_map(
        functools.partial(shards, mesh.shape["row"], mesh.shape["col"]),
        mesh=mesh,
        in_specs=(placed, placed, placed, P("groups")),
        out_specs=placed,
        check_vma=False,
    )
```

```python
import functools

import jax
import jax.numpy as jnp
from jax import lax
from jax.experimental import pallas as pl
from jax.experimental.pallas import tpu as pltpu
from jax.sharding import PartitionSpec as P

HEAD_DIM = 128
RATE = HEAD_DIM ** (-0.5) * 1.4426950408889634
MASKED = -1e30
AHEAD_SLOTS = 8


def kernel(
    n_row,
    n_col,
    lanes,
    reach,
    lens_ref,
    q_ref,
    k_ref,
    v_ref,
    o_ref,
    kbuf,
    vbuf,
    top_ref,
    total_ref,
    acc_ref,
    qa_ref,
    s_ref,
    load_sem,
    in_sem,
    mate_sem,
    up_send,
    cross_send,
    mate_send,
):
    shard = q_ref.shape[0]
    heads = q_ref.shape[1] // HEAD_DIM
    levels = n_row // lanes
    steps = 2 * (min(levels - 1, (reach + lanes - 1) // lanes) + 1)
    row = lax.axis_index("row")
    col = lax.axis_index("col")
    level = row // lanes
    lane = row % lanes
    mate = 1 - col
    other = level * lanes + (lanes - 1 - lane)
    mine = pl.ds(pl.multiple_of(col * shard, shard), shard)
    theirs = pl.ds(pl.multiple_of(mate * shard, shard), shard)

    def needs(reader, source):
        return (source >= 0) & (reader > source) & (reader - source <= reach)

    has_up = level + 1 < levels
    has_down = level > 0
    has_other = lanes > 1

    barrier = pltpu.get_barrier_semaphore()
    pl.semaphore_signal(barrier, inc=1, device_id={"col": mate})
    if has_other:
        pl.semaphore_signal(barrier, inc=1, device_id={"row": other})

    @pl.when(has_up)
    def _():
        pl.semaphore_signal(barrier, inc=1, device_id={"row": row + lanes})

    @pl.when(has_down)
    def _():
        pl.semaphore_signal(barrier, inc=1, device_id={"row": row - lanes})

    loads = [
        pltpu.make_async_copy(k_ref, kbuf.at[row, mine, :], load_sem.at[0]),
        pltpu.make_async_copy(v_ref, vbuf.at[row, mine, :], load_sem.at[1]),
    ]
    for head in range(heads):
        part = q_ref.at[:, head * HEAD_DIM : (head + 1) * HEAD_DIM]
        loads.append(
            pltpu.make_async_copy(part, qa_ref.at[head, :, :HEAD_DIM], load_sem.at[2 + head])
        )
    for load in loads:
        load.start()

    count = 1 + int(has_other) + has_up.astype(jnp.int32) + has_down.astype(jnp.int32)
    pl.semaphore_wait(barrier, count)

    def send(src, buf, source, which, j, sends, recvs, at, device):
        return pltpu.make_async_remote_copy(
            src_ref=src,
            dst_ref=buf.at[source, mine, :],
            send_sem=sends.at[which, j],
            recv_sem=recvs.at[which, at],
            device_id=device,
            device_id_type=pl.DeviceIdType.MESH,
        )

    def source_of(j):
        dist, kind = j // 2, j % 2
        cross = kind == 1
        from_lane = jnp.where(cross, lanes - 1 - lane, lane)
        source = (level - dist) * lanes + from_lane
        if lanes == 1:
            source = jnp.where(cross, -1, source)
        return source

    def relays(j, source, straight):
        mate_wants = (source < row) | (col < mate)
        found = [(mate_wants, mate_send, mate_sem, j, {"col": mate})]
        up = straight & has_up & needs(row + lanes, source)
        found.append((up, up_send, in_sem, j + 2, {"row": row + lanes}))
        if has_other:
            cross = straight & needs(other, source)
            found.append((cross, cross_send, in_sem, j + 1, {"row": other}))
        return found

    def forward(src, buf, source, which, j, straight):
        for wanted, sends, recvs, at, device in reversed(relays(j, source, straight)):

            @pl.when(wanted)
            def _():
                send(src, buf, source, which, j, sends, recvs, at, device).start()

    def arrived(buf, source, which, j, sems, part):
        here = buf.at[source, part, :]
        pltpu.make_async_copy(here, here, sems.at[which, j]).wait()

    forward(k_ref, kbuf, row, 0, 0, True)
    forward(v_ref, vbuf, row, 1, 0, True)

    first = (row * n_col + col) * shard
    qpos = first + lax.broadcasted_iota(jnp.int32, (1, shard), 1)

    def within(places):
        return (places >= begins) & (places < ends)

    lanes_of = lax.broadcasted_iota(jnp.int32, (1, HEAD_DIM), 1)
    begins = jnp.zeros((1, HEAD_DIM), jnp.int32)
    ends = jnp.full((1, HEAD_DIM), n_row * n_col * shard, jnp.int32)
    end = jnp.int32(0)
    docs = lens_ref.shape[0]
    for doc in range(docs):
        begins = jnp.where(lanes_of == doc, end, begins)
        end = end + lens_ref[doc]
        ends = jnp.where(lanes_of == doc, end, ends)
    qplace = first + lax.broadcasted_iota(jnp.int32, (shard, HEAD_DIM), 0)
    member = jnp.where(within(qplace) & (lanes_of < docs), 1.0, 0.0).astype(jnp.bfloat16)
    for head in range(heads):
        qa_ref[head, :, HEAD_DIM:] = member
    for load in loads:
        load.wait()

    def attend(kblock, vblock, kfirst, fresh):
        count = kblock.shape[0]
        kplace = kfirst + lax.broadcasted_iota(jnp.int32, (count, HEAD_DIM), 0)
        apart = jnp.where(within(kplace), 0.0, MASKED).astype(jnp.bfloat16)
        kwide = jnp.concatenate([kblock, apart], axis=1)
        if fresh:
            kpos = kfirst + lax.broadcasted_iota(jnp.int32, (count, shard), 0)
            bias = jnp.where(kpos <= qpos, jnp.float32(0.0), jnp.float32(MASKED))
        vflip = vblock.T

        def score(head):
            scores = lax.dot_general(
                kwide, qa_ref[head], (((1,), (1,)), ((), ())), preferred_element_type=jnp.float32
            )
            if fresh:
                scores = scores + bias
            s_ref[head % AHEAD_SLOTS, :count, :] = scores
            top = jnp.max(scores, axis=0, keepdims=True)
            if fresh:
                return top, top
            before = top_ref[head : head + 1, :]
            return before, jnp.maximum(before, top)

        tops = [score(head) for head in range(AHEAD_SLOTS - 1)]
        for head in range(heads):
            before, top = tops[head]
            if head + AHEAD_SLOTS - 1 < heads:
                tops.append(score(head + AHEAD_SLOTS - 1))
            weights = jnp.exp2((s_ref[head % AHEAD_SLOTS, :count, :] - top) * RATE)
            total = jnp.sum(weights, axis=0, keepdims=True)
            summed = jnp.dot(
                vflip, weights.astype(jnp.bfloat16), preferred_element_type=jnp.float32
            )
            if not fresh:
                factor = jnp.exp2((before - top) * RATE)
                total = total + total_ref[head : head + 1, :] * factor
                summed = summed + acc_ref[head] * factor
            top_ref[head : head + 1, :] = top
            total_ref[head : head + 1, :] = total
            acc_ref[head] = summed

    attend(kbuf[row, mine, :], vbuf[row, mine, :], first, True)

    def relay(j, least):
        source = source_of(j)

        @pl.when((j >= least) & (j < steps) & needs(row, source))
        def _():
            for which, buf in enumerate((kbuf, vbuf)):
                arrived(buf, source, which, j, in_sem, mine)
                forward(buf.at[source, mine, :], buf, source, which, j, j % 2 == 0)

    relay(jnp.int32(2), 1)
    relay(jnp.int32(1), 1)

    @pl.when(col > 0)
    def _():
        arrived(kbuf, row, 0, 0, mate_sem, theirs)
        arrived(vbuf, row, 1, 0, mate_sem, theirs)
        attend(kbuf[row, :shard, :], vbuf[row, :shard, :], row * n_col * shard, False)

    @pl.loop(1, steps)
    def _(j):
        source = source_of(j)

        @pl.when(needs(row, source))
        def _():
            arrived(kbuf, source, 0, j, mate_sem, theirs)
            arrived(vbuf, source, 1, j, mate_sem, theirs)
            attend(kbuf[source], vbuf[source], source * n_col * shard, False)

        ahead = 2 * (j - jnp.where(lane == lanes - 1, 0, 1)) + 1
        relay(ahead + 1, 3)
        relay(ahead, 3)

    for head in range(heads):
        inverse = 1.0 / total_ref[head : head + 1, :]
        result = (acc_ref[head] * inverse).T
        o_ref[:, head * HEAD_DIM : (head + 1) * HEAD_DIM] = result.astype(o_ref.dtype)

    @pl.loop(0, steps)
    def _(j):
        source = source_of(j)

        @pl.when(needs(row, source) | (j == 0))
        def _():
            for wanted, sends, recvs, at, device in relays(j, source, j % 2 == 0):

                @pl.when(wanted)
                def _():
                    for which, buf in enumerate((kbuf, vbuf)):
                        part = buf.at[source, mine, :]
                        send(part, buf, source, which, j, sends, recvs, at, device).wait_send()


def shards(n_row, n_col, queries, keys, values, doc_lengths):
    shard, width = queries.shape
    lanes = 2 if n_row % 2 == 0 else 1
    span = shard * n_row * n_col
    longest = (3 * span) // 4
    reach = min(n_row - 1, -(-longest // (shard * n_col)))
    levels = n_row // lanes
    steps = 2 * (min(levels - 1, (reach + lanes - 1) // lanes) + 1)
    tile = shard * n_col
    heads = width // HEAD_DIM
    vmem = pl.BlockSpec(memory_space=pltpu.VMEM)
    whole = pl.BlockSpec(memory_space=pltpu.HBM)
    sems = pltpu.SemaphoreType.DMA((2, steps))
    return pl.pallas_call(
        functools.partial(kernel, n_row, n_col, lanes, reach),
        out_shape=jax.ShapeDtypeStruct(queries.shape, queries.dtype),
        in_specs=[pl.BlockSpec(memory_space=pltpu.SMEM), whole, whole, whole],
        out_specs=vmem,
        scratch_shapes=[
            pltpu.VMEM((n_row, tile, HEAD_DIM), keys.dtype),
            pltpu.VMEM((n_row, tile, HEAD_DIM), values.dtype),
            pltpu.VMEM((heads, shard), jnp.float32),
            pltpu.VMEM((heads, shard), jnp.float32),
            pltpu.VMEM((heads, HEAD_DIM, shard), jnp.float32),
            pltpu.VMEM((heads, shard, 2 * HEAD_DIM), queries.dtype),
            pltpu.VMEM((AHEAD_SLOTS, tile, shard), jnp.float32),
            pltpu.SemaphoreType.DMA((2 + heads,)),
            sems,
            sems,
            sems,
            sems,
            sems,
        ],
        compiler_params=pltpu.CompilerParams(
            collective_id=0, has_side_effects=True, vmem_limit_bytes=24 << 20
        ),
        name="attend",
    )(*(pltpu.with_memory_space_constraint(x, pltpu.HBM) for x in (doc_lengths, queries, keys, values)))


def solution(mesh):
    placed = P(("groups", "row", "col"), None)
    return jax.shard_map(
        functools.partial(shards, mesh.shape["row"], mesh.shape["col"]),
        mesh=mesh,
        in_specs=(placed, placed, placed, P("groups")),
        out_specs=placed,
        check_vma=False,
    )
```
